512 devices in a mesh: ctx: 32 (over z, y_hi, core), fsdp: 16 (over y_lo, x).
Axes of the slice: x: 4, y: 8 (y_hi: 2, y_lo: 4; y = y_hi * 4 + y_lo), z: 8, core: 2. Of those that a mesh axis runs over, the one named last changes fastest.
Arguments:
- tokens: bfloat16 [16384, 8192], P('ctx', 'fsdp'), may hold values from -6 to 6
- gain: float32 [8192], replicated, may hold values from 0.5 to 1.5
- in_weight: bfloat16 [8192, 3, 4096], P('ctx', None, 'fsdp'), may hold values from -0.0625 to 0.0625
- short_filter: float32 [3, 3, 4096], P(None, None, 'fsdp'), may hold values from -3.5 to 3.5
- long_filter: float32 [128, 4096], P(None, 'fsdp'), may hold values from -0.5 to 0.5
Outputs:
- gated_out: bfloat16 [16384, 4096], P('ctx', 'fsdp')
The draws below stay inside these ranges and needn't reach their ends.
All inputs are finite; a program needn't handle non-finite values.
Results may differ from the reference program's by a relative error of at most 0.0086.
Values may be sent and summed in bfloat16 or wider, within the bound.
A program may use at most 64 MiB of HBM per device.

```python
import jax
import jax.numpy as jnp
from jax import lax

D = 8192
FILT = 128
SHORT = 3
CH = 4096
TOKENS = 16384


def block_scale(key, dims, shards, low, largest):
    loudness, own = 1.0, jax.random.fold_in(key, 6)
    for axis_at, shards_of in shards:
        heights = jnp.exp(jax.random.uniform(jax.random.fold_in(own, axis_at), (shards_of,), jnp.float32, low / len(shards), largest / len(shards)))
        loudness = loudness * jnp.repeat(heights, dims[axis_at] // shards_of).reshape([-1 if axis == axis_at else 1 for axis in range(len(dims))])
    return loudness


def scatter_about(rng, extent, deviation, reach, cuts=(), held_as=jnp.bfloat16):
    array = jax.random.normal(rng, extent, jnp.float32) * deviation
    if len(cuts) > 0:
        array = block_scale(rng, extent, cuts, -0.22, 0.18) * array
    return jnp.clip(array, min=-reach, max=reach).astype(held_as)


def setup_inputs(seed: int = 0) -> dict:
    splits = jax.random.split(jax.random.key(seed), 6)
    return {
        "tokens": scatter_about(splits[0], (TOKENS, D), 1.0, 6.0, ((0, 32), (1, 16))),
        "gain": jnp.clip(1.0 + 0.1 * jax.random.normal(splits[1], (D,), jnp.float32), 0.5, 1.5),
        "in_weight": scatter_about(splits[2], (D, 3, CH), D ** -0.5, 0.0625, ((0, 32), (2, 16))),
        "short_filter": scatter_about(splits[3], (SHORT, 3, CH), SHORT ** -0.5, 3.5, ((2, 16),), jnp.float32),
        "long_filter": scatter_about(splits[4], (FILT, CH), FILT ** -0.5, 0.5, ((1, 16),), jnp.float32),
    }


def reference(tokens, gain, in_weight, short_filter, long_filter):
    widened = tokens.astype(jnp.float32)
    mean_square = lax.optimization_barrier(jnp.mean(widened * widened, axis=1, keepdims=True))
    normed = (widened * lax.rsqrt(mean_square + 1e-06) * gain).astype(jnp.bfloat16)
    total_rows = tokens.shape[0]
    channels = in_weight.shape[2]
    projected = jnp.dot(normed, in_weight.reshape(in_weight.shape[0], 3 * channels), preferred_element_type=jnp.float32).astype(jnp.bfloat16)
    short_taps = short_filter.reshape(SHORT, 3 * channels)
    padded = jnp.concatenate([jnp.zeros((SHORT - 1, 3 * channels), jnp.float32), projected.astype(jnp.float32)], axis=0)
    featurized = jnp.zeros((total_rows, 3 * channels), jnp.float32)
    for offset in range(SHORT):
        featurized = featurized + short_taps[offset] * padded[SHORT - 1 - offset:SHORT - 1 - offset + total_rows]
    query = featurized[:, :channels]
    keyed = featurized[:, channels:2 * channels]
    valued = featurized[:, 2 * channels:]
    gated = (keyed * valued).astype(jnp.bfloat16)
    signal = jnp.concatenate([jnp.zeros((FILT - 1, channels), jnp.float32), gated.astype(jnp.float32)], axis=0)
    response = jnp.zeros((total_rows, channels), jnp.float32)
    for offset in range(FILT):
        response = response + long_filter[offset] * signal[FILT - 1 - offset:FILT - 1 - offset + total_rows]
    return (query * response).astype(jnp.bfloat16)
```

```python
import jax
import jax.numpy as jnp
from jax import lax
from jax.experimental import pallas as pl
from jax.experimental.pallas import tpu as pltpu
from jax.sharding import PartitionSpec as P

MESH = pl.DeviceIdType.MESH
F32 = jnp.float32
BF16 = jnp.bfloat16

ROWS, FEATS, KROWS, CHAN = 512, 512, 256, 256
TAPS, SHORT = 128, 3


def kernel(tok, gain, w, sfilt, lfilt, out, tall, wall, acc, ssq, pf, gext, gsh, gsend, psend, grecv, precv,
           lsem, tss, trs, wss, wrs, hss, hrs):
    ctx = lax.axis_index("ctx")
    fsdp = lax.axis_index("fsdp")
    core = ctx % 2
    hi = (ctx // 2) % 2
    z = ctx // 4
    x = fsdp % 4
    lo = fsdp // 4

    def at(xx, ll, hh, zz, cc):
        return ((zz * 2 + hh) * 2 + cc, ll * 4 + xx)

    xp, xm = at((x + 1) % 4, lo, hi, z, core), at((x + 3) % 4, lo, hi, z, core)
    zp, zm = at(x, lo, hi, (z + 1) % 8, core), at(x, lo, hi, (z + 7) % 8, core)
    y = hi * 4 + lo
    yp = at(x, (y + 1) % 8 % 4, (y + 1) % 8 // 4, z, core)
    ym = at(x, (y + 7) % 8 % 4, (y + 7) % 8 // 4, z, core)
    partner = at(x, lo, 1 - hi, z, core)
    sibling = at(x, lo, hi, z, 1 - core)
    following = ((ctx + 1) % 32, fsdp)
    previous = ((ctx + 31) % 32, fsdp)

    barrier = pltpu.get_barrier_semaphore()
    for d in (xp, xm, yp, ym, zp, zm, partner, sibling, previous):
        pl.semaphore_signal(barrier, inc=1, device_id=d, device_id_type=MESH)
    pl.semaphore_wait(barrier, 9)

    def tslice(ref, half):
        return ref.at[pl.ds(half * 256, 256)]

    def tcopy(j, half, way, dest, src=None):
        src = tall.at[j] if src is None else src
        return pltpu.make_async_remote_copy(
            src_ref=tslice(src, half), dst_ref=tslice(tall.at[j], half),
            send_sem=tss.at[j, half, way], recv_sem=trs.at[j, half],
            device_id=dest, device_id_type=MESH)

    def twait(j, half):
        tcopy(j, half, 0, xp).wait_recv()

    me_t = lo * 4 + x
    sent_sign = 3 - 2 * lo
    cols = [lo, lo + 1 - 2 * (lo % 2), 2 - lo // 2, 3 - 3 * (lo // 2)]
    middle = (lo == 1) | (lo == 2)

    def own_y(start):
        @pl.when(lo < 3)
        def _():
            for half in range(2):
                c = tcopy(me_t, half, 2, yp, tok)
                c.start() if start else c.wait_send()

        @pl.when(lo > 0)
        def _():
            for half in range(2):
                c = tcopy(me_t, half, 3, ym, tok)
                c.start() if start else c.wait_send()

    def along_x(n, half, start):
        j = cols[n] * 4 + x
        src = tok if n == 0 else None
        for way, dest in ((0, xp), (1, xm)):
            c = tcopy(j, half, way, dest, src)
            c.start() if start else c.wait_send()

    def forward_y(n, half, start):
        j = cols[n] * 4 + x
        sign = sent_sign if n == 1 else -sent_sign

        @pl.when(middle)
        def _():
            dest = at(x, lo + sign, hi, z, core)
            c = tcopy(j, half, 2, dest)
            c.start() if start else c.wait_send()

    def forward_x(n, half, start):
        if half == 0:
            c = tcopy(cols[n] * 4 + (x + 3) % 4, 0, 0, xp)
        else:
            c = tcopy(cols[n] * 4 + (x + 1) % 4, 1, 1, xm)
        c.start() if start else c.wait_send()

    def wfull(i):
        return wall.at[i // 2, pl.ds(pl.multiple_of((i % 2) * 256, 256), 256)]

    def wslice(i, half):
        return wall.at[i // 2, pl.ds(pl.multiple_of((i % 2) * 256 + half * 128, 128), 128)]

    def wcopy(i, half, way, dest):
        return pltpu.make_async_remote_copy(
            src_ref=wslice(i, half), dst_ref=wslice(i, half),
            send_sem=wss.at[i, half, way], recv_sem=wrs.at[i, half],
            device_id=dest, device_id_type=MESH)

    def wsib(i):
        return pltpu.make_async_remote_copy(
            src_ref=wfull(i), dst_ref=wfull(i), send_sem=wss.at[i, 0, 2], recv_sem=wrs.at[i, 0],
            device_id=sibling, device_id_type=MESH)

    def wid(stream, distance):
        hh = hi if stream == 0 else 1 - hi
        return (((z + 8 + distance) % 8) * 2 + hh) * 2 + core

    def along_z(stream, k, start):
        for half in range(2):
            if k <= 2 or half == 0:
                c = wcopy(wid(stream, -k), half, 0, zp)
                c.start() if start else c.wait_send()
            if k <= 2 or half == 1:
                c = wcopy(wid(stream, k), half, 1, zm)
                c.start() if start else c.wait_send()

    def z_arrived(stream, k):
        for half in range(2):
            if k < 4 or half == 0:
                wcopy(wid(stream, -k), half, 0, zp).wait_recv()
            if k < 4 or half == 1:
                wcopy(wid(stream, k), half, 1, zm).wait_recv()

    def to_sibling(stream, k, start):
        for distance in sorted({-k, k}) if k < 4 else (4,):
            c = wsib(wid(stream, distance))
            c.start() if start else c.wait_send()

    local = pltpu.make_async_copy(tok, tall.at[me_t], lsem)
    local.start()
    own_y(True)
    for half in range(2):
        along_x(0, half, True)
    for b in range(3):
        wall[ctx // 2, pl.ds(pl.multiple_of(core * 256, 256), 256), b * 256:(b + 1) * 256] = w[:, b, :]
    along_z(0, 0, True)
    to_sibling(0, 0, True)
    for half in range(2):
        wcopy(ctx, half, 3, partner).start()

    def w_step(stream, k):
        z_arrived(stream, k)
        if k < 4:
            along_z(stream, k, True)
        to_sibling(stream, k, True)

    def y_step(n):
        for half in range(2):
            twait(cols[n] * 4 + x, half)
            forward_y(n, half, True)
            along_x(n, half, True)

    def x_step(n):
        twait(cols[n] * 4 + (x + 3) % 4, 0)
        forward_x(n, 0, True)
        twait(cols[n] * 4 + (x + 1) % 4, 1)
        forward_x(n, 1, True)

    w_step(0, 1)
    x_step(0)
    y_step(1)
    w_step(0, 2)
    y_step(2)
    w_step(0, 3)
    x_step(1)
    w_step(0, 4)
    for half in range(2):
        wcopy(wid(1, 0), half, 3, partner).wait_recv()
    along_z(1, 0, True)
    to_sibling(1, 0, True)
    y_step(3)
    w_step(1, 1)
    x_step(2)
    w_step(1, 2)
    w_step(1, 3)
    w_step(1, 4)
    x_step(3)
    for n in range(4):
        twait(cols[n] * 4 + (x + 3) % 4, 1)
        twait(cols[n] * 4 + (x + 1) % 4, 0)
        twait(cols[n] * 4 + (x + 2) % 4, 0)
        twait(cols[n] * 4 + (x + 2) % 4, 1)

    def sib_wait(m, carry):
        i = m * 2 + 1 - core
        wsib(i).wait_recv()
        return carry

    lax.fori_loop(0, 16, sib_wait, 0)
    local.wait()

    acc[...] = jnp.zeros_like(acc)
    ssq[...] = jnp.zeros_like(ssq)

    def chunk(j, carry):
        raw = tall[j].astype(F32)
        sq = raw * raw
        ssq[...] += (sq[:, 0:128] + sq[:, 128:256]) + (sq[:, 256:384] + sq[:, 384:512])
        scaled = (raw * gain[pl.ds(j, 1), :]).astype(BF16)
        acc[...] += jnp.dot(scaled, wall[j], preferred_element_type=F32)
        return carry

    lax.fori_loop(0, 16, chunk, 0)

    scale = lax.rsqrt(jnp.sum(ssq[...], axis=1, keepdims=True) * (1.0 / 8192) + 1e-6)
    projected = (acc[...] * scale).astype(BF16)
    psend[...] = projected[496:512]
    pf[8:520, :] = projected.astype(F32)

    def mixed(start, count, b):
        total = None
        for s in range(SHORT):
            term = sfilt[s, b:b + 1, :] * pf[8 + start - s:8 + start - s + count, b * 256:(b + 1) * 256]
            total = term if total is None else total + term
        return total

    tail = (mixed(384, 128, 1) * mixed(384, 128, 2)).astype(BF16)
    gsend[...] = tail

    def halo(k):
        src, dst = ((gsend, grecv), (psend, precv))[k]
        return pltpu.make_async_remote_copy(
            src_ref=src, dst_ref=dst, send_sem=hss.at[k], recv_sem=hrs.at[k],
            device_id=following, device_id_type=MESH)

    @pl.when(ctx < 31)
    def _():
        halo(0).start()
        halo(1).start()

    @pl.when(ctx > 0)
    def _():
        halo(0).wait_recv()
        halo(1).wait_recv()

    @pl.when(ctx == 0)
    def _():
        grecv[...] = jnp.zeros_like(grecv)
        precv[...] = jnp.zeros_like(precv)

    pf[0:8, :] = precv[8:16, :].astype(F32)
    gext[8:136, :] = grecv[...].astype(F32)
    gext[136:648, :] = (mixed(0, 512, 1) * mixed(0, 512, 2)).astype(BF16).astype(F32)
    query = mixed(0, 512, 0)
    acc[:, 0:256] = query

    for b in range(8):
        gsh[b] = gext[8 - b:648 - b, :]

    def conv(step, carry):
        row = pl.multiple_of((step // 2) * 64, 64)
        lanes = pl.ds(pl.multiple_of((step % 2) * 128, 128), 128)
        total = jnp.zeros((64, 128), F32)
        for b in range(8):
            window = gsh[b, pl.ds(row + 8, 184), lanes]
            for a in range(16):
                total = total + lfilt[8 * a + b:8 * a + b + 1, lanes] * window[8 * (15 - a):8 * (15 - a) + 64]
        out[pl.ds(row, 64), lanes] = (acc[pl.ds(row, 64), lanes] * total).astype(BF16)
        return carry

    lax.fori_loop(0, 16, conv, 0)

    own_y(False)
    for n in range(4):
        for half in range(2):
            along_x(n, half, False)
            forward_x(n, half, False)
            if n > 0:
                forward_y(n, half, False)
    for stream in range(2):
        for k in range(5):
            if k < 4:
                along_z_wait(along_z, stream, k)
            to_sibling(stream, k, False)
    for half in range(2):
        wcopy(ctx, half, 3, partner).wait_send()

    @pl.when(ctx < 31)
    def _():
        halo(0).wait_send()
        halo(1).wait_send()


def along_z_wait(along_z, stream, k):
    along_z(stream, k, False)


def on_device(tokens, gain, in_weight, short_filter, long_filter):
    vmem = pl.BlockSpec(memory_space=pltpu.VMEM)
    dma = pltpu.SemaphoreType.DMA
    return pl.pallas_call(
        kernel,
        out_shape=jax.ShapeDtypeStruct((ROWS, CHAN), BF16),
        in_specs=[pl.BlockSpec(memory_space=pl.ANY), vmem, vmem, vmem, vmem],
        out_specs=vmem,
        scratch_shapes=[
            pltpu.VMEM((16, ROWS, FEATS), BF16),
            pltpu.VMEM((16, 512, 3 * CHAN), BF16),
            pltpu.VMEM((ROWS, 3 * CHAN), F32),
            pltpu.VMEM((ROWS, 128), F32),
            pltpu.VMEM((ROWS + 8, 3 * CHAN), F32),
            pltpu.VMEM((ROWS + 136, CHAN), F32),
            pltpu.VMEM((8, ROWS + 128, CHAN), F32),
            pltpu.VMEM((128, CHAN), BF16),
            pltpu.VMEM((16, 3 * CHAN), BF16),
            pltpu.VMEM((128, CHAN), BF16),
            pltpu.VMEM((16, 3 * CHAN), BF16),
            dma,
            dma((16, 2, 4)),
            dma((16, 2)),
            dma((32, 2, 4)),
            dma((32, 2)),
            dma((2,)),
            dma((2,)),
        ],
        name="hyena",
        compiler_params=pltpu.CompilerParams(
            collective_id=0, has_side_effects=True, vmem_limit_bytes=56 << 20),
    )(tokens, gain.reshape(16, 512), in_weight, short_filter, long_filter)


def solution(mesh):
    return jax.shard_map(
        on_device,
        mesh=mesh,
        in_specs=(
            P("ctx", "fsdp"),
            P(),
            P("ctx", None, "fsdp"),
            P(None, None, "fsdp"),
            P(None, "fsdp"),
        ),
        out_specs=P("ctx", "fsdp"),
        check_vma=False,
    )
```

```python
import jax
import jax.numpy as jnp
from jax import lax
from jax.experimental import pallas as pl
from jax.experimental.pallas import tpu as pltpu
from jax.sharding import PartitionSpec as P

MESH = pl.DeviceIdType.MESH
F32 = jnp.float32
BF16 = jnp.bfloat16

ROWS, FEATS, KROWS, CHAN = 512, 512, 256, 256
TAPS, SHORT = 128, 3


def kernel(tok, gain, w, sfilt, lfilt, out, tall, wall, acc, ssq, pf, gext, gsh, gsend, psend, grecv, precv,
           lsem, tss, trs, wss, wrs, hss, hrs):
    ctx = lax.axis_index("ctx")
    fsdp = lax.axis_index("fsdp")
    core = ctx % 2
    hi = (ctx // 2) % 2
    z = ctx // 4
    x = fsdp % 4
    lo = fsdp // 4

    def at(xx, ll, hh, zz, cc):
        return ((zz * 2 + hh) * 2 + cc, ll * 4 + xx)

    xp, xm = at((x + 1) % 4, lo, hi, z, core), at((x + 3) % 4, lo, hi, z, core)
    zp, zm = at(x, lo, hi, (z + 1) % 8, core), at(x, lo, hi, (z + 7) % 8, core)
    y = hi * 4 + lo
    yp = at(x, (y + 1) % 8 % 4, (y + 1) % 8 // 4, z, core)
    ym = at(x, (y + 7) % 8 % 4, (y + 7) % 8 // 4, z, core)
    partner = at(x, lo, 1 - hi, z, core)
    sibling = at(x, lo, hi, z, 1 - core)
    following = ((ctx + 1) % 32, fsdp)
    previous = ((ctx + 31) % 32, fsdp)

    barrier = pltpu.get_barrier_semaphore()
    for d in (xp, xm, yp, ym, zp, zm, partner, sibling, previous):
        pl.semaphore_signal(barrier, inc=1, device_id=d, device_id_type=MESH)
    pl.semaphore_wait(barrier, 9)

    def tslice(ref, half):
        return ref.at[pl.ds(half * 256, 256)]

    def tcopy(j, half, way, dest, src=None):
        src = tall.at[j] if src is None else src
        return pltpu.make_async_remote_copy(
            src_ref=tslice(src, half), dst_ref=tslice(tall.at[j], half),
            send_sem=tss.at[j, half, way], recv_sem=trs.at[j, half],
            device_id=dest, device_id_type=MESH)

    def twait(j, half):
        tcopy(j, half, 0, xp).wait_recv()

    me_t = lo * 4 + x
    sent_sign = 3 - 2 * lo
    cols = [lo, lo + 1 - 2 * (lo % 2), 2 - lo // 2, 3 - 3 * (lo // 2)]
    middle = (lo == 1) | (lo == 2)

    def own_y(half, start):
        @pl.when(lo < 3)
        def _():
            c = tcopy(me_t, half, 2, yp, tok)
            c.start() if start else c.wait_send()

        @pl.when(lo > 0)
        def _():
            c = tcopy(me_t, half, 3, ym, tok)
            c.start() if start else c.wait_send()

    def along_x(n, half, start):
        j = cols[n] * 4 + x
        src = tok if n == 0 else None
        for way, dest in ((0, xp), (1, xm)):
            c = tcopy(j, half, way, dest, src)
            c.start() if start else c.wait_send()

    def forward_y(n, half, start):
        j = cols[n] * 4 + x
        sign = sent_sign if n == 1 else -sent_sign

        @pl.when(middle)
        def _():
            dest = at(x, lo + sign, hi, z, core)
            c = tcopy(j, half, 2, dest)
            c.start() if start else c.wait_send()

    def forward_x(n, half, start):
        if half == 0:
            c = tcopy(cols[n] * 4 + (x + 3) % 4, 0, 0, xp)
        else:
            c = tcopy(cols[n] * 4 + (x + 1) % 4, 1, 1, xm)
        c.start() if start else c.wait_send()

    def wpart(i, half):
        return wall.at[i // 2, :, pl.ds(pl.multiple_of((i % 2) * 256 + half * 128, 128), 128)]

    def wfull(i):
        return wall.at[i // 2, :, pl.ds(pl.multiple_of((i % 2) * 256, 256), 256)]

    def wcopy(i, half, way, dest, own=False):
        return pltpu.make_async_remote_copy(
            src_ref=w.at[:, pl.ds(half * 128, 128)] if own else wpart(i, half), dst_ref=wpart(i, half),
            send_sem=wss.at[i, half, way], recv_sem=wrs.at[i, half],
            device_id=dest, device_id_type=MESH)

    def wsib(i, own=False):
        return pltpu.make_async_remote_copy(
            src_ref=w if own else wfull(i), dst_ref=wfull(i), send_sem=wss.at[i, 0, 2], recv_sem=wrs.at[i, 0],
            device_id=sibling, device_id_type=MESH)

    def wid(stream, distance):
        hh = hi if stream == 0 else 1 - hi
        return (((z + 8 + distance) % 8) * 2 + hh) * 2 + core

    def along_z(stream, k, half, start):
        own = stream == 0 and k == 0
        if k <= 2 or half == 0:
            c = wcopy(wid(stream, -k), half, 0, zp, own)
            c.start() if start else c.wait_send()
        if k <= 2 or half == 1:
            c = wcopy(wid(stream, k), half, 1, zm, own)
            c.start() if start else c.wait_send()

    def to_sibling(stream, k, start):
        for distance in sorted({-k, k}) if k < 4 else (4,):
            c = wsib(wid(stream, distance), stream == 0 and k == 0)
            c.start() if start else c.wait_send()

    def to_partner(half, start):
        c = wcopy(ctx, half, 3, partner, True)
        c.start() if start else c.wait_send()

    local_t = pltpu.make_async_copy(tok, tall.at[me_t], lsem.at[0])
    local_w = pltpu.make_async_copy(w, wfull(ctx), lsem.at[1])

    def w_step(stream, k, half):
        if k < 4 or half == 0:
            wcopy(wid(stream, -k), half, 0, zp).wait_recv()
            if k <= 2 or (k == 3 and half == 0):
                wcopy(wid(stream, -k), half, 0, zp).start()
        if k < 4 or half == 1:
            wcopy(wid(stream, k), half, 1, zm).wait_recv()
            if k <= 2 or (k == 3 and half == 1):
                wcopy(wid(stream, k), half, 1, zm).start()
        if half == 1:
            to_sibling(stream, k, True)

    def p_step(half):
        wcopy(wid(1, 0), half, 3, partner).wait_recv()
        along_z(1, 0, half, True)
        if half == 1:
            to_sibling(1, 0, True)

    def y_step(n, half):
        twait(cols[n] * 4 + x, half)
        forward_y(n, half, True)
        along_x(n, half, True)

    def x_step(n, half):
        twait(cols[n] * 4 + ((x + 3) % 4 if half == 0 else (x + 1) % 4), half)
        forward_x(n, half, True)

    def column_done(n):
        twait(cols[n] * 4 + (x + 3) % 4, 1)
        twait(cols[n] * 4 + (x + 1) % 4, 0)
        twait(cols[n] * 4 + (x + 2) % 4, 0)
        twait(cols[n] * 4 + (x + 2) % 4, 1)

    def siblings_done(stream):
        hh = hi if stream == 0 else 1 - hi

        def one(m, carry):
            wsib((m * 2 + hh) * 2 + 1 - core).wait_recv()
            return carry

        lax.fori_loop(0, 8, one, 0)

    def chunk(j):
        raw = tall[j].astype(F32)
        sq = raw * raw
        ssq[...] += (sq[:, 0:128] + sq[:, 128:256]) + (sq[:, 256:384] + sq[:, 384:512])
        scaled = (raw * gain[:, pl.ds(pl.multiple_of(j * 512, 512), 512)]).astype(BF16)
        for b in range(3):
            acc[:, b * 256:(b + 1) * 256] += jnp.dot(scaled, wall[j, b], preferred_element_type=F32)

    def products(n, stream):
        hh = hi if stream == 0 else 1 - hi

        def one(m, carry):
            chunk(cols[n] * 4 + hh + 2 * m)
            return carry

        lax.fori_loop(0, 2, one, 0)

    for half in range(2):
        along_z(0, 0, half, True)
        along_x(0, half, True)
        own_y(half, True)
    to_sibling(0, 0, True)
    local_t.start()
    local_w.start()
    acc[...] = jnp.zeros_like(acc)
    ssq[...] = jnp.zeros_like(ssq)

    w_step(0, 1, 0)
    x_step(0, 0)
    y_step(1, 0)
    w_step(0, 1, 1)
    w_step(0, 2, 0)
    x_step(0, 1)
    y_step(1, 1)
    to_partner(0, True)
    w_step(0, 2, 1)
    y_step(2, 0)
    w_step(0, 3, 0)
    y_step(2, 1)
    to_partner(1, True)
    x_step(1, 0)
    w_step(0, 3, 1)
    x_step(1, 1)
    w_step(0, 4, 0)
    w_step(0, 4, 1)
    local_t.wait()
    local_w.wait()
    column_done(0)
    siblings_done(0)
    products(0, 0)
    p_step(0)
    y_step(3, 0)
    p_step(1)
    column_done(1)
    products(1, 0)
    w_step(1, 1, 0)
    y_step(3, 1)
    w_step(1, 1, 1)
    x_step(2, 0)
    w_step(1, 2, 0)
    x_step(2, 1)
    w_step(1, 2, 1)
    column_done(2)
    products(2, 0)
    w_step(1, 3, 0)
    w_step(1, 3, 1)
    x_step(3, 0)
    w_step(1, 4, 0)
    w_step(1, 4, 1)
    siblings_done(1)
    products(0, 1)
    products(1, 1)
    x_step(3, 1)
    products(2, 1)
    column_done(3)
    products(3, 0)
    products(3, 1)

    scale = lax.rsqrt(jnp.sum(ssq[...], axis=1, keepdims=True) * (1.0 / 8192) + 1e-6)
    projected = (acc[...] * scale).astype(BF16)
    psend[...] = projected[496:512]
    pf[8:520, :] = projected.astype(F32)

    def mixed(start, count, b):
        total = None
        for s in range(SHORT):
            term = sfilt[s, b:b + 1, :] * pf[8 + start - s:8 + start - s + count, b * 256:(b + 1) * 256]
            total = term if total is None else total + term
        return total

    tail = (mixed(384, 128, 1) * mixed(384, 128, 2)).astype(BF16)
    gsend[...] = tail

    def halo(k):
        src, dst = ((gsend, grecv), (psend, precv))[k]
        return pltpu.make_async_remote_copy(
            src_ref=src, dst_ref=dst, send_sem=hss.at[k], recv_sem=hrs.at[k],
            device_id=following, device_id_type=MESH)

    @pl.when(ctx < 31)
    def _():
        halo(0).start()
        halo(1).start()

    @pl.when(ctx > 0)
    def _():
        halo(0).wait_recv()
        halo(1).wait_recv()

    @pl.when(ctx == 0)
    def _():
        grecv[...] = jnp.zeros_like(grecv)
        precv[...] = jnp.zeros_like(precv)

    pf[0:8, :] = precv[8:16, :].astype(F32)
    gext[8:136, :] = grecv[...].astype(F32)
    gext[136:648, :] = (mixed(0, 512, 1) * mixed(0, 512, 2)).astype(BF16).astype(F32)
    query = mixed(0, 512, 0)
    acc[:, 0:256] = query

    for b in range(8):
        gsh[b] = gext[8 - b:648 - b, :]

    def conv(step, carry):
        row = pl.multiple_of((step // 2) * 64, 64)
        lanes = pl.ds(pl.multiple_of((step % 2) * 128, 128), 128)
        total = jnp.zeros((64, 128), F32)
        for b in range(8):
            window = gsh[b, pl.ds(row + 8, 184), lanes]
            for a in range(16):
                total = total + lfilt[8 * a + b:8 * a + b + 1, lanes] * window[8 * (15 - a):8 * (15 - a) + 64]
        out[pl.ds(row, 64), lanes] = (acc[pl.ds(row, 64), lanes] * total).astype(BF16)
        return carry

    lax.fori_loop(0, 16, conv, 0)

    for half in range(2):
        own_y(half, False)
        to_partner(half, False)
        for n in range(4):
            along_x(n, half, False)
            forward_x(n, half, False)
            if n > 0:
                forward_y(n, half, False)
        for stream in range(2):
            for k in range(4):
                along_z(stream, k, half, False)
    for stream in range(2):
        for k in range(5):
            to_sibling(stream, k, False)

    @pl.when(ctx < 31)
    def _():
        halo(0).wait_send()
        halo(1).wait_send()


def on_device(tokens, gain, in_weight, short_filter, long_filter):
    vmem = pl.BlockSpec(memory_space=pltpu.VMEM)
    anywhere = pl.BlockSpec(memory_space=pl.ANY)
    dma = pltpu.SemaphoreType.DMA
    return pl.pallas_call(
        kernel,
        out_shape=jax.ShapeDtypeStruct((ROWS, CHAN), BF16),
        in_specs=[anywhere, vmem, anywhere, vmem, vmem],
        out_specs=vmem,
        scratch_shapes=[
            pltpu.VMEM((16, ROWS, FEATS), BF16),
            pltpu.VMEM((16, 3, 512, CHAN), BF16),
            pltpu.VMEM((ROWS, 3 * CHAN), F32),
            pltpu.VMEM((ROWS, 128), F32),
            pltpu.VMEM((ROWS + 8, 3 * CHAN), F32),
            pltpu.VMEM((ROWS + 136, CHAN), F32),
            pltpu.VMEM((8, ROWS + 128, CHAN), F32),
            pltpu.VMEM((128, CHAN), BF16),
            pltpu.VMEM((16, 3 * CHAN), BF16),
            pltpu.VMEM((128, CHAN), BF16),
            pltpu.VMEM((16, 3 * CHAN), BF16),
            dma((2,)),
            dma((16, 2, 4)),
            dma((16, 2)),
            dma((32, 2, 4)),
            dma((32, 2)),
            dma((2,)),
            dma((2,)),
        ],
        name="hyena",
        compiler_params=pltpu.CompilerParams(
            collective_id=0, has_side_effects=True, vmem_limit_bytes=56 << 20),
    )(tokens, gain.reshape(1, 8192), in_weight.transpose(1, 0, 2), short_filter, long_filter)


def solution(mesh):
    return jax.shard_map(
        on_device,
        mesh=mesh,
        in_specs=(
            P("ctx", "fsdp"),
            P(),
            P("ctx", None, "fsdp"),
            P(None, None, "fsdp"),
            P(None, "fsdp"),
        ),
        out_specs=P("ctx", "fsdp"),
        check_vma=False,
    )
```

```python
import jax
import jax.numpy as jnp
from jax import lax
from jax.experimental import pallas as pl
from jax.experimental.pallas import tpu as pltpu
from jax.sharding import PartitionSpec as P

MESH = pl.DeviceIdType.MESH
F32 = jnp.float32
BF16 = jnp.bfloat16

ROWS, FEATS, KROWS, CHAN = 512, 512, 256, 256
TAPS, SHORT = 128, 3


def split_taps(values):
    pairs = values.reshape(values.shape[0] // 2, 2, 8, CHAN)
    even, odd = pairs[:, 0], pairs[:, 1]
    return [odd, even + odd, even]


def split_tiles(tiles, count):
    def tile(s):
        return tiles[s + count - 1]

    at = range(1 - count // 2, (len(tiles) - count + 1) // 2)
    return [[tile(2 * m - 1) - tile(2 * m) for m in at], [tile(2 * m) for m in at],
            [tile(2 * m + 1) - tile(2 * m) for m in at]]


def joined(parts):
    result = []
    for before, both, after in zip(*parts):
        result += [both + before, both + after]
    return result


def kernel(tok, gain, w, sfilt, lfilt, out, tall, wall, acc, ssq, pf, gext, gsh, taps, gsend, psend, grecv, precv,
           lsem, tss, trs, wss, wrs, hss, hrs):
    ctx = lax.axis_index("ctx")
    fsdp = lax.axis_index("fsdp")
    core = ctx % 2
    hi = (ctx // 2) % 2
    z = ctx // 4
    x = fsdp % 4
    lo = fsdp // 4

    def at(xx, ll, hh, zz, cc):
        return ((zz * 2 + hh) * 2 + cc, ll * 4 + xx)

    xp, xm = at((x + 1) % 4, lo, hi, z, core), at((x + 3) % 4, lo, hi, z, core)
    zp, zm = at(x, lo, hi, (z + 1) % 8, core), at(x, lo, hi, (z + 7) % 8, core)
    y = hi * 4 + lo
    yp = at(x, (y + 1) % 8 % 4, (y + 1) % 8 // 4, z, core)
    ym = at(x, (y + 7) % 8 % 4, (y + 7) % 8 // 4, z, core)
    partner = at(x, lo, 1 - hi, z, core)
    sibling = at(x, lo, hi, z, 1 - core)
    following = ((ctx + 1) % 32, fsdp)
    previous = ((ctx + 31) % 32, fsdp)

    barrier = pltpu.get_barrier_semaphore()
    for d in (xp, xm, yp, ym, zp, zm, partner, sibling, previous):
        pl.semaphore_signal(barrier, inc=1, device_id=d, device_id_type=MESH)
    pl.semaphore_wait(barrier, 9)

    def tslice(ref, half):
        return ref.at[pl.ds(half * 256, 256)]

    def tcopy(j, half, way, dest, src=None):
        src = tall.at[j] if src is None else src
        return pltpu.make_async_remote_copy(
            src_ref=tslice(src, half), dst_ref=tslice(tall.at[j], half),
            send_sem=tss.at[j, half, way], recv_sem=trs.at[j, half],
            device_id=dest, device_id_type=MESH)

    def twait(j, half):
        tcopy(j, half, 0, xp).wait_recv()

    me_t = lo * 4 + x
    sent_sign = 3 - 2 * lo
    cols = [lo, lo + 1 - 2 * (lo % 2), 2 - lo // 2, 3 - 3 * (lo // 2)]
    middle = (lo == 1) | (lo == 2)

    def own_y(half, start):
        @pl.when(lo < 3)
        def _():
            c = tcopy(me_t, half, 2, yp, tok)
            c.start() if start else c.wait_send()

        @pl.when(lo > 0)
        def _():
            c = tcopy(me_t, half, 3, ym, tok)
            c.start() if start else c.wait_send()

    def along_x(n, half, start):
        j = cols[n] * 4 + x
        src = tok if n == 0 else None
        for way, dest in ((0, xp), (1, xm)):
            c = tcopy(j, half, way, dest, src)
            c.start() if start else c.wait_send()

    def forward_y(n, half, start):
        j = cols[n] * 4 + x
        sign = sent_sign if n == 1 else -sent_sign

        @pl.when(middle)
        def _():
            dest = at(x, lo + sign, hi, z, core)
            c = tcopy(j, half, 2, dest)
            c.start() if start else c.wait_send()

    def forward_x(n, half, start):
        if half == 0:
            c = tcopy(cols[n] * 4 + (x + 3) % 4, 0, 0, xp)
        else:
            c = tcopy(cols[n] * 4 + (x + 1) % 4, 1, 1, xm)
        c.start() if start else c.wait_send()

    def wpart(i, half):
        return wall.at[i // 2, :, pl.ds(pl.multiple_of((i % 2) * 256 + half * 128, 128), 128)]

    def wfull(i):
        return wall.at[i // 2, :, pl.ds(pl.multiple_of((i % 2) * 256, 256), 256)]

    def wcopy(i, half, way, dest, own=False):
        return pltpu.make_async_remote_copy(
            src_ref=w.at[:, pl.ds(half * 128, 128)] if own else wpart(i, half), dst_ref=wpart(i, half),
            send_sem=wss.at[i, half, way], recv_sem=wrs.at[i, half],
            device_id=dest, device_id_type=MESH)

    def wsib(i, own=False):
        return pltpu.make_async_remote_copy(
            src_ref=w if own else wfull(i), dst_ref=wfull(i), send_sem=wss.at[i, 0, 2], recv_sem=wrs.at[i, 0],
            device_id=sibling, device_id_type=MESH)

    def wid(stream, distance):
        hh = hi if stream == 0 else 1 - hi
        return (((z + 8 + distance) % 8) * 2 + hh) * 2 + core

    def along_z(stream, k, half, start):
        own = stream == 0 and k == 0
        if k <= 2 or half == 0:
            c = wcopy(wid(stream, -k), half, 0, zp, own)
            c.start() if start else c.wait_send()
        if k <= 2 or half == 1:
            c = wcopy(wid(stream, k), half, 1, zm, own)
            c.start() if start else c.wait_send()

    def to_sibling(stream, k, start):
        for distance in sorted({-k, k}) if k < 4 else (4,):
            c = wsib(wid(stream, distance), stream == 0 and k == 0)
            c.start() if start else c.wait_send()

    def to_partner(half, start):
        c = wcopy(ctx, half, 3, partner, True)
        c.start() if start else c.wait_send()

    local_t = pltpu.make_async_copy(tok, tall.at[me_t], lsem.at[0])
    local_w = pltpu.make_async_copy(w, wfull(ctx), lsem.at[1])

    def w_step(stream, k, half):
        if k < 4 or half == 0:
            wcopy(wid(stream, -k), half, 0, zp).wait_recv()
            if k <= 2 or (k == 3 and half == 0):
                wcopy(wid(stream, -k), half, 0, zp).start()
        if k < 4 or half == 1:
            wcopy(wid(stream, k), half, 1, zm).wait_recv()
            if k <= 2 or (k == 3 and half == 1):
                wcopy(wid(stream, k), half, 1, zm).start()
        if half == 1:
            to_sibling(stream, k, True)

    def p_step(half):
        wcopy(wid(1, 0), half, 3, partner).wait_recv()
        along_z(1, 0, half, True)
        if half == 1:
            to_sibling(1, 0, True)

    def y_step(n, half):
        twait(cols[n] * 4 + x, half)
        forward_y(n, half, True)
        along_x(n, half, True)

    def x_step(n, half):
        twait(cols[n] * 4 + ((x + 3) % 4 if half == 0 else (x + 1) % 4), half)
        forward_x(n, half, True)

    def column_done(n):
        twait(cols[n] * 4 + (x + 3) % 4, 1)
        twait(cols[n] * 4 + (x + 1) % 4, 0)
        twait(cols[n] * 4 + (x + 2) % 4, 0)
        twait(cols[n] * 4 + (x + 2) % 4, 1)

    def siblings_done(stream):
        hh = hi if stream == 0 else 1 - hi

        def one(m, carry):
            wsib((m * 2 + hh) * 2 + 1 - core).wait_recv()
            return carry

        lax.fori_loop(0, 8, one, 0)

    def chunk(j):
        raw = tall[j].astype(F32)
        sq = raw * raw
        ssq[...] += (sq[:, 0:128] + sq[:, 128:256]) + (sq[:, 256:384] + sq[:, 384:512])
        scaled = (raw * gain[:, pl.ds(pl.multiple_of(j * 512, 512), 512)]).astype(BF16)
        for b in range(3):
            acc[:, b * 256:(b + 1) * 256] += jnp.dot(scaled, wall[j, b], preferred_element_type=F32)

    def products(n, stream):
        hh = hi if stream == 0 else 1 - hi

        def one(m, carry):
            chunk(cols[n] * 4 + hh + 2 * m)
            return carry

        lax.fori_loop(0, 2, one, 0)

    for half in range(2):
        if half == 1:
            along_z(0, 0, 0, False)
            along_x(0, 0, False)
        along_z(0, 0, half, True)
        along_x(0, half, True)
        if half == 1:
            own_y(0, False)
        own_y(half, True)
    to_partner(0, True)
    to_sibling(0, 0, True)
    local_t.start()
    local_w.start()
    acc[...] = jnp.zeros_like(acc)
    ssq[...] = jnp.zeros_like(ssq)
    for i, outer in enumerate(split_taps(lfilt[...].reshape(16, 8, CHAN))):
        for j, inner in enumerate(split_taps(outer)):
            taps[i * 3 + j] = inner

    w_step(0, 1, 0)
    x_step(0, 0)
    y_step(1, 0)
    w_step(0, 1, 1)
    w_step(0, 2, 0)
    x_step(0, 1)
    y_step(1, 1)
    w_step(0, 2, 1)
    y_step(2, 0)
    w_step(0, 3, 0)
    y_step(2, 1)
    to_partner(1, True)
    x_step(1, 0)
    w_step(0, 3, 1)
    x_step(1, 1)
    w_step(0, 4, 0)
    w_step(0, 4, 1)
    local_t.wait()
    local_w.wait()
    column_done(0)
    siblings_done(0)
    products(0, 0)
    p_step(0)
    y_step(3, 0)
    p_step(1)
    column_done(1)
    products(1, 0)
    w_step(1, 1, 0)
    y_step(3, 1)
    w_step(1, 1, 1)
    x_step(2, 0)
    w_step(1, 2, 0)
    x_step(2, 1)
    w_step(1, 2, 1)
    column_done(2)
    products(2, 0)
    w_step(1, 3, 0)
    w_step(1, 3, 1)
    x_step(3, 0)
    w_step(1, 4, 0)
    w_step(1, 4, 1)
    siblings_done(1)
    products(0, 1)
    products(1, 1)
    x_step(3, 1)
    products(2, 1)
    column_done(3)
    products(3, 0)
    products(3, 1)

    scale = lax.rsqrt(jnp.sum(ssq[...], axis=1, keepdims=True) * (1.0 / 8192) + 1e-6)
    projected = (acc[...] * scale).astype(BF16)
    psend[...] = projected[496:512]
    pf[8:520, :] = projected.astype(F32)

    def mixed(start, count, b):
        total = None
        for s in range(SHORT):
            term = sfilt[s, b:b + 1, :] * pf[8 + start - s:8 + start - s + count, b * 256:(b + 1) * 256]
            total = term if total is None else total + term
        return total

    tail = (mixed(384, 128, 1) * mixed(384, 128, 2)).astype(BF16)
    gsend[...] = tail

    def halo(k):
        src, dst = ((gsend, grecv), (psend, precv))[k]
        return pltpu.make_async_remote_copy(
            src_ref=src, dst_ref=dst, send_sem=hss.at[k], recv_sem=hrs.at[k],
            device_id=following, device_id_type=MESH)

    @pl.when(ctx < 31)
    def _():
        halo(0).start()
        halo(1).start()

    @pl.when(ctx > 0)
    def _():
        halo(0).wait_recv()
        halo(1).wait_recv()

    @pl.when(ctx == 0)
    def _():
        grecv[...] = jnp.zeros_like(grecv)
        precv[...] = jnp.zeros_like(precv)

    pf[0:8, :] = precv[8:16, :].astype(F32)
    gext[8:136, :] = grecv[...].astype(F32)
    gext[136:648, :] = (mixed(0, 512, 1) * mixed(0, 512, 2)).astype(BF16).astype(F32)
    query = mixed(0, 512, 0)
    acc[:, 0:256] = query

    for b in range(8):
        gsh[b] = gext[8 - b:648 - b, :]

    def conv(step, carry):
        row = pl.multiple_of((step // 2) * 128, 128)
        lanes = pl.ds(pl.multiple_of((step % 2) * 128, 128), 128)
        merged = []
        for i in range(3):
            sums = [[None] * 4 for _ in range(3)]
            for b in range(8):
                window = gsh[b, pl.ds(row + 8, 248), lanes]
                tiles = [window[8 * t:8 * t + 8] for t in range(31)]
                for j, part in enumerate(split_tiles(split_tiles(tiles, 16)[i], 8)):
                    for c in range(4):
                        weight = taps[i * 3 + j, c, b:b + 1, lanes]
                        for m in range(4):
                            term = weight * part[m + 3 - c]
                            sums[j][m] = term if sums[j][m] is None else sums[j][m] + term
            merged.append(joined(sums))
        response = jnp.concatenate(joined(merged), axis=0)
        out[pl.ds(row, 128), lanes] = (acc[pl.ds(row, 128), lanes] * response).astype(BF16)
        return carry

    lax.fori_loop(0, 8, conv, 0)

    for half in range(2):
        if half == 1:
            own_y(half, False)
        to_partner(half, False)
        for n in range(4):
            if n > 0 or half == 1:
                along_x(n, half, False)
            forward_x(n, half, False)
            if n > 0:
                forward_y(n, half, False)
        for stream in range(2):
            for k in range(4):
                if stream + k + half > 0:
                    along_z(stream, k, half, False)
    for stream in range(2):
        for k in range(5):
            to_sibling(stream, k, False)

    @pl.when(ctx < 31)
    def _():
        halo(0).wait_send()
        halo(1).wait_send()


def on_device(tokens, gain, in_weight, short_filter, long_filter):
    vmem = pl.BlockSpec(memory_space=pltpu.VMEM)
    anywhere = pl.BlockSpec(memory_space=pl.ANY)
    dma = pltpu.SemaphoreType.DMA
    return pl.pallas_call(
        kernel,
        out_shape=jax.ShapeDtypeStruct((ROWS, CHAN), BF16),
        in_specs=[anywhere, vmem, anywhere, vmem, vmem],
        out_specs=vmem,
        scratch_shapes=[
            pltpu.VMEM((16, ROWS, FEATS), BF16),
            pltpu.VMEM((16, 3, 512, CHAN), BF16),
            pltpu.VMEM((ROWS, 3 * CHAN), F32),
            pltpu.VMEM((ROWS, 128), F32),
            pltpu.VMEM((ROWS + 8, 3 * CHAN), F32),
            pltpu.VMEM((ROWS + 136, CHAN), F32),
            pltpu.VMEM((8, ROWS + 128, CHAN), F32),
            pltpu.VMEM((9, 4, 8, CHAN), F32),
            pltpu.VMEM((128, CHAN), BF16),
            pltpu.VMEM((16, 3 * CHAN), BF16),
            pltpu.VMEM((128, CHAN), BF16),
            pltpu.VMEM((16, 3 * CHAN), BF16),
            dma((2,)),
            dma((16, 2, 4)),
            dma((16, 2)),
            dma((32, 2, 4)),
            dma((32, 2)),
            dma((2,)),
            dma((2,)),
        ],
        name="hyena",
        compiler_params=pltpu.CompilerParams(
            collective_id=0, has_side_effects=True, vmem_limit_bytes=56 << 20),
    )(tokens, gain.reshape(1, 8192), in_weight.transpose(1, 0, 2), short_filter, long_filter)


def solution(mesh):
    return jax.shard_map(
        on_device,
        mesh=mesh,
        in_specs=(
            P("ctx", "fsdp"),
            P(),
            P("ctx", None, "fsdp"),
            P(None, None, "fsdp"),
            P(None, "fsdp"),
        ),
        out_specs=P("ctx", "fsdp"),
        check_vma=False,
    )
```

```python
import jax
import jax.numpy as jnp
from jax import lax
from jax.experimental import pallas as pl
from jax.experimental.pallas import tpu as pltpu
from jax.sharding import PartitionSpec as P

MESH = pl.DeviceIdType.MESH
F32 = jnp.float32
BF16 = jnp.bfloat16

ROWS, FEATS, KROWS, CHAN = 512, 512, 256, 256
TAPS, SHORT = 128, 3


def split_taps(values):
    pairs = values.reshape(values.shape[0] // 2, 2, 8, CHAN)
    even, odd = pairs[:, 0], pairs[:, 1]
    return [odd, even + odd, even]


def split_tiles(tiles, count):
    def tile(s):
        return tiles[s + count - 1]

    at = range(1 - count // 2, (len(tiles) - count + 1) // 2)
    return [[tile(2 * m - 1) - tile(2 * m) for m in at], [tile(2 * m) for m in at],
            [tile(2 * m + 1) - tile(2 * m) for m in at]]


def joined(parts):
    result = []
    for before, both, after in zip(*parts):
        result += [both + before, both + after]
    return result


def kernel(tok, gain, w, sfilt, lfilt, out, tall, scaled, wall, acc, ssq, pf, gext, gsh, taps, gsend, psend, grecv, precv,
           lsem, tss, trs, wss, wrs, hss, hrs):
    ctx = lax.axis_index("ctx")
    fsdp = lax.axis_index("fsdp")
    core = ctx % 2
    hi = (ctx // 2) % 2
    z = ctx // 4
    x = fsdp % 4
    lo = fsdp // 4

    def at(xx, ll, hh, zz, cc):
        return ((zz * 2 + hh) * 2 + cc, ll * 4 + xx)

    xp, xm = at((x + 1) % 4, lo, hi, z, core), at((x + 3) % 4, lo, hi, z, core)
    zp, zm = at(x, lo, hi, (z + 1) % 8, core), at(x, lo, hi, (z + 7) % 8, core)
    y = hi * 4 + lo
    yp = at(x, (y + 1) % 8 % 4, (y + 1) % 8 // 4, z, core)
    ym = at(x, (y + 7) % 8 % 4, (y + 7) % 8 // 4, z, core)
    partner = at(x, lo, 1 - hi, z, core)
    sibling = at(x, lo, hi, z, 1 - core)
    following = ((ctx + 1) % 32, fsdp)
    previous = ((ctx + 31) % 32, fsdp)

    barrier = pltpu.get_barrier_semaphore()
    for d in (xp, xm, yp, ym, zp, zm, partner, sibling, previous):
        pl.semaphore_signal(barrier, inc=1, device_id=d, device_id_type=MESH)
    pl.semaphore_wait(barrier, 9)

    def tslice(ref, half):
        return ref.at[pl.ds(half * 256, 256)]

    def tcopy(j, half, way, dest, src=None):
        src = tall.at[j] if src is None else src
        return pltpu.make_async_remote_copy(
            src_ref=tslice(src, half), dst_ref=tslice(tall.at[j], half),
            send_sem=tss.at[j, half, way], recv_sem=trs.at[j, half],
            device_id=dest, device_id_type=MESH)

    def twait(j, half):
        tcopy(j, half, 0, xp).wait_recv()

    me_t = lo * 4 + x
    sent_sign = 3 - 2 * lo
    cols = [lo, lo + 1 - 2 * (lo % 2), 2 - lo // 2, 3 - 3 * (lo // 2)]
    middle = (lo == 1) | (lo == 2)

    def own_y(half, start):
        @pl.when(lo < 3)
        def _():
            c = tcopy(me_t, half, 2, yp, tok)
            c.start() if start else c.wait_send()

        @pl.when(lo > 0)
        def _():
            c = tcopy(me_t, half, 3, ym, tok)
            c.start() if start else c.wait_send()

    def along_x(n, half, start):
        j = cols[n] * 4 + x
        src = tok if n == 0 else None
        for way, dest in ((0, xp), (1, xm)):
            c = tcopy(j, half, way, dest, src)
            c.start() if start else c.wait_send()

    def forward_y(n, half, start):
        j = cols[n] * 4 + x
        sign = sent_sign if n == 1 else -sent_sign

        @pl.when(middle)
        def _():
            dest = at(x, lo + sign, hi, z, core)
            c = tcopy(j, half, 2, dest)
            c.start() if start else c.wait_send()

    def forward_x(n, half, start):
        if half == 0:
            c = tcopy(cols[n] * 4 + (x + 3) % 4, 0, 0, xp)
        else:
            c = tcopy(cols[n] * 4 + (x + 1) % 4, 1, 1, xm)
        c.start() if start else c.wait_send()

    def wpart(i, half):
        return wall.at[i // 2, :, pl.ds(pl.multiple_of((i % 2) * 256 + half * 128, 128), 128)]

    def wfull(i):
        return wall.at[i // 2, :, pl.ds(pl.multiple_of((i % 2) * 256, 256), 256)]

    def wcopy(i, half, way, dest, own=False):
        return pltpu.make_async_remote_copy(
            src_ref=w.at[:, pl.ds(half * 128, 128)] if own else wpart(i, half), dst_ref=wpart(i, half),
            send_sem=wss.at[i, half, way], recv_sem=wrs.at[i, half],
            device_id=dest, device_id_type=MESH)

    def wsib(i, own=False):
        return pltpu.make_async_remote_copy(
            src_ref=w if own else wfull(i), dst_ref=wfull(i), send_sem=wss.at[i, 0, 2], recv_sem=wrs.at[i, 0],
            device_id=sibling, device_id_type=MESH)

    def wid(stream, distance):
        hh = hi if stream == 0 else 1 - hi
        return (((z + 8 + distance) % 8) * 2 + hh) * 2 + core

    def along_z(stream, k, half, start):
        own = stream == 0 and k == 0
        if k <= 2 or half == 0:
            c = wcopy(wid(stream, -k), half, 0, zp, own)
            c.start() if start else c.wait_send()
        if k <= 2 or half == 1:
            c = wcopy(wid(stream, k), half, 1, zm, own)
            c.start() if start else c.wait_send()

    def to_sibling(stream, k, start):
        for distance in sorted({-k, k}) if k < 4 else (4,):
            c = wsib(wid(stream, distance), stream == 0 and k == 0)
            c.start() if start else c.wait_send()

    def to_partner(half, start):
        c = wcopy(ctx, half, 3, partner, True)
        c.start() if start else c.wait_send()

    local_t = pltpu.make_async_copy(tok, tall.at[me_t], lsem.at[0])
    local_w = pltpu.make_async_copy(w, wfull(ctx), lsem.at[1])

    def w_step(stream, k, half):
        if k < 4 or half == 0:
            wcopy(wid(stream, -k), half, 0, zp).wait_recv()
            if k <= 2 or (k == 3 and half == 0):
                wcopy(wid(stream, -k), half, 0, zp).start()
        if k < 4 or half == 1:
            wcopy(wid(stream, k), half, 1, zm).wait_recv()
            if k <= 2 or (k == 3 and half == 1):
                wcopy(wid(stream, k), half, 1, zm).start()
        if half == 1:
            to_sibling(stream, k, True)

    def p_step(half):
        wcopy(wid(1, 0), half, 3, partner).wait_recv()
        along_z(1, 0, half, True)
        if half == 1:
            to_sibling(1, 0, True)

    def y_step(n, half):
        twait(cols[n] * 4 + x, half)
        forward_y(n, half, True)
        along_x(n, half, True)

    def x_step(n, half):
        twait(cols[n] * 4 + ((x + 3) % 4 if half == 0 else (x + 1) % 4), half)
        forward_x(n, half, True)

    def column_done(n):
        twait(cols[n] * 4 + (x + 3) % 4, 1)
        twait(cols[n] * 4 + (x + 1) % 4, 0)
        twait(cols[n] * 4 + (x + 2) % 4, 0)
        twait(cols[n] * 4 + (x + 2) % 4, 1)

    def siblings_done(stream):
        hh = hi if stream == 0 else 1 - hi

        def one(m, carry):
            wsib((m * 2 + hh) * 2 + 1 - core).wait_recv()
            return carry

        lax.fori_loop(0, 8, one, 0)

    def scale_column(n):
        def one(m, carry):
            j = cols[n] * 4 + m
            raw = tall[j].astype(F32)
            sq = raw * raw
            ssq[...] += (sq[:, 0:128] + sq[:, 128:256]) + (sq[:, 256:384] + sq[:, 384:512])
            scaled[j] = (raw * gain[:, pl.ds(pl.multiple_of(j * 512, 512), 512)]).astype(BF16)
            return carry

        lax.fori_loop(0, 4, one, 0)

    def products(n, stream):
        hh = hi if stream == 0 else 1 - hi
        first = cols[n] * 4 + hh
        for b in range(3):
            acc[:, b * 256:(b + 1) * 256] += (
                jnp.dot(scaled[first], wall[first, b], preferred_element_type=F32)
                + jnp.dot(scaled[first + 2], wall[first + 2, b], preferred_element_type=F32))

    for half in range(2):
        if half == 1:
            along_z(0, 0, 0, False)
            along_x(0, 0, False)
        along_z(0, 0, half, True)
        along_x(0, half, True)
        if half == 1:
            own_y(0, False)
        own_y(half, True)
    to_partner(0, True)
    to_sibling(0, 0, True)
    local_t.start()
    local_w.start()
    acc[...] = jnp.zeros_like(acc)
    ssq[...] = jnp.zeros_like(ssq)
    for i, outer in enumerate(split_taps(lfilt[...].reshape(16, 8, CHAN))):
        for j, inner in enumerate(split_taps(outer)):
            taps[i * 3 + j] = inner

    w_step(0, 1, 0)
    x_step(0, 0)
    y_step(1, 0)
    w_step(0, 1, 1)
    x_step(0, 1)
    y_step(1, 1)
    w_step(0, 2, 0)
    y_step(2, 0)
    w_step(0, 2, 1)
    w_step(0, 3, 0)
    x_step(1, 0)
    y_step(2, 1)
    w_step(0, 3, 1)
    x_step(1, 1)
    to_partner(1, True)
    p_step(0)
    w_step(0, 4, 0)
    w_step(0, 4, 1)
    local_t.wait()
    local_w.wait()
    column_done(0)
    scale_column(0)
    siblings_done(0)
    products(0, 0)
    y_step(3, 0)
    p_step(1)
    column_done(1)
    scale_column(1)
    products(1, 0)
    w_step(1, 1, 0)
    y_step(3, 1)
    x_step(2, 0)
    w_step(1, 1, 1)
    w_step(1, 2, 0)
    x_step(2, 1)
    w_step(1, 2, 1)
    column_done(2)
    scale_column(2)
    products(2, 0)
    w_step(1, 3, 0)
    w_step(1, 3, 1)
    x_step(3, 0)
    x_step(3, 1)
    w_step(1, 4, 0)
    w_step(1, 4, 1)
    siblings_done(1)
    products(0, 1)
    products(1, 1)
    products(2, 1)
    column_done(3)
    scale_column(3)
    products(3, 0)
    products(3, 1)

    scale = lax.rsqrt(jnp.sum(ssq[...], axis=1, keepdims=True) * (1.0 / 8192) + 1e-6)
    projected = (acc[...] * scale).astype(BF16)
    psend[...] = projected[496:512]
    pf[8:520, :] = projected.astype(F32)

    def mixed(start, count, b):
        total = None
        for s in range(SHORT):
            term = sfilt[s, b:b + 1, :] * pf[8 + start - s:8 + start - s + count, b * 256:(b + 1) * 256]
            total = term if total is None else total + term
        return total

    tail = (mixed(384, 128, 1) * mixed(384, 128, 2)).astype(BF16)
    gsend[...] = tail

    def halo(k):
        src, dst = ((gsend, grecv), (psend, precv))[k]
        return pltpu.make_async_remote_copy(
            src_ref=src, dst_ref=dst, send_sem=hss.at[k], recv_sem=hrs.at[k],
            device_id=following, device_id_type=MESH)

    @pl.when(ctx < 31)
    def _():
        halo(0).start()
        halo(1).start()

    def gate(start, count):
        return (mixed(start, count, 1) * mixed(start, count, 2)).astype(BF16).astype(F32)

    gext[144:648, :] = gate(8, 504)
    acc[8:512, 0:256] = mixed(8, 504, 0)
    for b in range(8):
        gsh[b, 144:640] = gext[152 - b:648 - b, :]

    def conv(step, carry):
        row = pl.multiple_of((step // 2) * 128, 128)
        lanes = pl.ds(pl.multiple_of((step % 2) * 128, 128), 128)
        merged = []
        for i in range(3):
            sums = [[None] * 4 for _ in range(3)]
            for b in range(8):
                window = gsh[b, pl.ds(row + 8, 248), lanes]
                tiles = [window[8 * t:8 * t + 8] for t in range(31)]
                for j, part in enumerate(split_tiles(split_tiles(tiles, 16)[i], 8)):
                    for c in range(4):
                        weight = taps[i * 3 + j, c, b:b + 1, lanes]
                        for m in range(4):
                            term = weight * part[m + 3 - c]
                            sums[j][m] = term if sums[j][m] is None else sums[j][m] + term
            merged.append(joined(sums))
        response = jnp.concatenate(joined(merged), axis=0)
        out[pl.ds(row, 128), lanes] = (acc[pl.ds(row, 128), lanes] * response).astype(BF16)
        return carry

    lax.fori_loop(4, 8, conv, 0)

    @pl.when(ctx > 0)
    def _():
        halo(0).wait_recv()
        halo(1).wait_recv()

    @pl.when(ctx == 0)
    def _():
        grecv[...] = jnp.zeros_like(grecv)
        precv[...] = jnp.zeros_like(precv)

    pf[0:8, :] = precv[8:16, :].astype(F32)
    gext[8:136, :] = grecv[...].astype(F32)
    gext[136:144, :] = gate(0, 8)
    acc[0:8, 0:256] = mixed(0, 8, 0)
    for b in range(8):
        gsh[b, 0:144] = gext[8 - b:152 - b, :]

    lax.fori_loop(0, 4, conv, 0)

    for half in range(2):
        if half == 1:
            own_y(half, False)
        to_partner(half, False)
        for n in range(4):
            if n > 0 or half == 1:
                along_x(n, half, False)
            forward_x(n, half, False)
            if n > 0:
                forward_y(n, half, False)
        for stream in range(2):
            for k in range(4):
                if stream + k + half > 0:
                    along_z(stream, k, half, False)
    for stream in range(2):
        for k in range(5):
            to_sibling(stream, k, False)

    @pl.when(ctx < 31)
    def _():
        halo(0).wait_send()
        halo(1).wait_send()


def on_device(tokens, gain, in_weight, short_filter, long_filter):
    vmem = pl.BlockSpec(memory_space=pltpu.VMEM)
    anywhere = pl.BlockSpec(memory_space=pl.ANY)
    dma = pltpu.SemaphoreType.DMA
    return pl.pallas_call(
        kernel,
        out_shape=jax.ShapeDtypeStruct((ROWS, CHAN), BF16),
        in_specs=[anywhere, vmem, anywhere, vmem, vmem],
        out_specs=vmem,
        scratch_shapes=[
            pltpu.VMEM((16, ROWS, FEATS), BF16),
            pltpu.VMEM((16, ROWS, FEATS), BF16),
            pltpu.VMEM((16, 3, 512, CHAN), BF16),
            pltpu.VMEM((ROWS, 3 * CHAN), F32),
            pltpu.VMEM((ROWS, 128), F32),
            pltpu.VMEM((ROWS + 8, 3 * CHAN), F32),
            pltpu.VMEM((ROWS + 136, CHAN), F32),
            pltpu.VMEM((8, ROWS + 128, CHAN), F32),
            pltpu.VMEM((9, 4, 8, CHAN), F32),
            pltpu.VMEM((128, CHAN), BF16),
            pltpu.VMEM((16, 3 * CHAN), BF16),
            pltpu.VMEM((128, CHAN), BF16),
            pltpu.VMEM((16, 3 * CHAN), BF16),
            dma((2,)),
            dma((16, 2, 4)),
            dma((16, 2)),
            dma((32, 2, 4)),
            dma((32, 2)),
            dma((2,)),
            dma((2,)),
        ],
        name="hyena",
        compiler_params=pltpu.CompilerParams(
            collective_id=0, has_side_effects=True, vmem_limit_bytes=56 << 20),
    )(tokens, gain.reshape(1, 8192), in_weight.transpose(1, 0, 2), short_filter, long_filter)


def solution(mesh):
    return jax.shard_map(
        on_device,
        mesh=mesh,
        in_specs=(
            P("ctx", "fsdp"),
            P(),
            P("ctx", None, "fsdp"),
            P(None, None, "fsdp"),
            P(None, "fsdp"),
        ),
        out_specs=P("ctx", "fsdp"),
        check_vma=False,
    )
```

```python
import jax
import jax.numpy as jnp
from jax import lax
from jax.experimental import pallas as pl
from jax.experimental.pallas import tpu as pltpu
from jax.sharding import PartitionSpec as P

MESH = pl.DeviceIdType.MESH
F32 = jnp.float32
BF16 = jnp.bfloat16

ROWS, FEATS, KROWS, CHAN = 512, 512, 256, 256
TAPS, SHORT = 128, 3


def split_taps(values):
    pairs = values.reshape(values.shape[0] // 2, 2, 8, CHAN)
    even, odd = pairs[:, 0], pairs[:, 1]
    return [odd, even + odd, even]


def split_tiles(tiles, count):
    def tile(s):
        return tiles[s + count - 1]

    at = range(1 - count // 2, (len(tiles) - count + 1) // 2)
    return [[tile(2 * m - 1) - tile(2 * m) for m in at], [tile(2 * m) for m in at],
            [tile(2 * m + 1) - tile(2 * m) for m in at]]


def joined(parts):
    result = []
    for before, both, after in zip(*parts):
        result += [both + before, both + after]
    return result


def kernel(tok, gain, w, sfilt, lfilt, out, tall, scaled, wall, acc, ssq, pf, gext, gsh, taps, gsend, psend, grecv, precv,
           lsem, tss, trs, wss, wrs, hss, hrs):
    ctx = lax.axis_index("ctx")
    fsdp = lax.axis_index("fsdp")
    core = ctx % 2
    hi = (ctx // 2) % 2
    z = ctx // 4
    x = fsdp % 4
    lo = fsdp // 4

    def at(xx, ll, hh, zz, cc):
        return ((zz * 2 + hh) * 2 + cc, ll * 4 + xx)

    xp, xm = at((x + 1) % 4, lo, hi, z, core), at((x + 3) % 4, lo, hi, z, core)
    zp, zm = at(x, lo, hi, (z + 1) % 8, core), at(x, lo, hi, (z + 7) % 8, core)
    y = hi * 4 + lo
    yp = at(x, (y + 1) % 8 % 4, (y + 1) % 8 // 4, z, core)
    ym = at(x, (y + 7) % 8 % 4, (y + 7) % 8 // 4, z, core)
    partner = at(x, lo, 1 - hi, z, core)
    sibling = at(x, lo, hi, z, 1 - core)
    following = ((ctx + 1) % 32, fsdp)
    previous = ((ctx + 31) % 32, fsdp)

    barrier = pltpu.get_barrier_semaphore()
    for d in (xp, xm, yp, ym, zp, zm, partner, sibling, previous):
        pl.semaphore_signal(barrier, inc=1, device_id=d, device_id_type=MESH)
    pl.semaphore_wait(barrier, 9)

    def tslice(ref, half):
        return ref.at[pl.ds(half * 256, 256)]

    def tcopy(j, half, way, dest, src=None):
        src = tall.at[j] if src is None else src
        return pltpu.make_async_remote_copy(
            src_ref=tslice(src, half), dst_ref=tslice(tall.at[j], half),
            send_sem=tss.at[j, half, way], recv_sem=trs.at[j, half],
            device_id=dest, device_id_type=MESH)

    def twait(j, half):
        tcopy(j, half, 0, xp).wait_recv()

    me_t = lo * 4 + x
    sent_sign = 3 - 2 * lo
    cols = [lo, lo + 1 - 2 * (lo % 2), 2 - lo // 2, 3 - 3 * (lo // 2)]
    middle = (lo == 1) | (lo == 2)

    def own_y(half, start):
        @pl.when(lo < 3)
        def _():
            c = tcopy(me_t, half, 2, yp, tok)
            c.start() if start else c.wait_send()

        @pl.when(lo > 0)
        def _():
            c = tcopy(me_t, half, 3, ym, tok)
            c.start() if start else c.wait_send()

    def along_x(n, half, start):
        j = cols[n] * 4 + x
        src = tok if n == 0 else None
        for way, dest in ((0, xp), (1, xm)):
            c = tcopy(j, half, way, dest, src)
            c.start() if start else c.wait_send()

    def forward_y(n, half, start):
        j = cols[n] * 4 + x
        sign = sent_sign if n == 1 else -sent_sign

        @pl.when(middle)
        def _():
            dest = at(x, lo + sign, hi, z, core)
            c = tcopy(j, half, 2, dest)
            c.start() if start else c.wait_send()

    def forward_x(n, half, start):
        if half == 0:
            c = tcopy(cols[n] * 4 + (x + 3) % 4, 0, 0, xp)
        else:
            c = tcopy(cols[n] * 4 + (x + 1) % 4, 1, 1, xm)
        c.start() if start else c.wait_send()

    def wpart(i, half):
        return wall.at[i // 2, :, pl.ds(pl.multiple_of((i % 2) * 256 + half * 128, 128), 128)]

    def wfull(i):
        return wall.at[i // 2, :, pl.ds(pl.multiple_of((i % 2) * 256, 256), 256)]

    def wcopy(i, half, way, dest, own=False):
        return pltpu.make_async_remote_copy(
            src_ref=w.at[:, pl.ds(half * 128, 128)] if own else wpart(i, half), dst_ref=wpart(i, half),
            send_sem=wss.at[i, half, way], recv_sem=wrs.at[i, half],
            device_id=dest, device_id_type=MESH)

    def wsib(i, own=False):
        return pltpu.make_async_remote_copy(
            src_ref=w if own else wfull(i), dst_ref=wfull(i), send_sem=wss.at[i, 0, 2], recv_sem=wrs.at[i, 0],
            device_id=sibling, device_id_type=MESH)

    def wid(stream, distance):
        hh = hi if stream == 0 else 1 - hi
        return (((z + 8 + distance) % 8) * 2 + hh) * 2 + core

    def along_z(stream, k, half, start):
        own = stream == 0 and k == 0
        if k <= 2 or half == 0:
            c = wcopy(wid(stream, -k), half, 0, zp, own)
            c.start() if start else c.wait_send()
        if k <= 2 or half == 1:
            c = wcopy(wid(stream, k), half, 1, zm, own)
            c.start() if start else c.wait_send()

    def to_sibling(stream, k, start):
        for distance in sorted({-k, k}) if k < 4 else (4,):
            c = wsib(wid(stream, distance), stream == 0 and k == 0)
            c.start() if start else c.wait_send()

    def to_partner(half, start):
        c = wcopy(ctx, half, 3, partner, True)
        c.start() if start else c.wait_send()

    local_t = pltpu.make_async_copy(tok, tall.at[me_t], lsem.at[0])
    local_w = pltpu.make_async_copy(w, wfull(ctx), lsem.at[1])

    def w_step(stream, k, half):
        if k < 4 or half == 0:
            wcopy(wid(stream, -k), half, 0, zp).wait_recv()
            if k <= 2 or (k == 3 and half == 0):
                wcopy(wid(stream, -k), half, 0, zp).start()
        if k < 4 or half == 1:
            wcopy(wid(stream, k), half, 1, zm).wait_recv()
            if k <= 2 or (k == 3 and half == 1):
                wcopy(wid(stream, k), half, 1, zm).start()
        if half == 1:
            to_sibling(stream, k, True)

    def p_step(half):
        wcopy(wid(1, 0), half, 3, partner).wait_recv()
        along_z(1, 0, half, True)
        if half == 1:
            to_sibling(1, 0, True)

    def y_step(n, half):
        twait(cols[n] * 4 + x, half)
        forward_y(n, half, True)
        along_x(n, half, True)

    def x_step(n, half):
        twait(cols[n] * 4 + ((x + 3) % 4 if half == 0 else (x + 1) % 4), half)
        forward_x(n, half, True)

    def column_done(n):
        twait(cols[n] * 4 + (x + 3) % 4, 1)
        twait(cols[n] * 4 + (x + 1) % 4, 0)
        twait(cols[n] * 4 + (x + 2) % 4, 0)
        twait(cols[n] * 4 + (x + 2) % 4, 1)

    def siblings_done(stream):
        hh = hi if stream == 0 else 1 - hi

        def one(m, carry):
            wsib((m * 2 + hh) * 2 + 1 - core).wait_recv()
            return carry

        lax.fori_loop(0, 8, one, 0)

    def scale_column(n):
        def one(m, carry):
            j = cols[n] * 4 + m
            raw = tall[j].astype(F32)
            sq = raw * raw
            ssq[...] += (sq[:, 0:128] + sq[:, 128:256]) + (sq[:, 256:384] + sq[:, 384:512])
            scaled[j] = (raw * gain[:, pl.ds(pl.multiple_of(j * 512, 512), 512)]).astype(BF16)
            return carry

        lax.fori_loop(0, 4, one, 0)

    def products(n, stream):
        hh = hi if stream == 0 else 1 - hi
        first = cols[n] * 4 + hh
        for b in range(3):
            acc[:, b * 256:(b + 1) * 256] += (
                jnp.dot(scaled[first], wall[first, b], preferred_element_type=F32)
                + jnp.dot(scaled[first + 2], wall[first + 2, b], preferred_element_type=F32))

    for half in range(2):
        if half == 1:
            along_z(0, 0, 0, False)
            along_x(0, 0, False)
        along_z(0, 0, half, True)
        along_x(0, half, True)
        if half == 1:
            own_y(0, False)
        own_y(half, True)
    to_partner(0, True)
    to_sibling(0, 0, True)
    local_t.start()
    local_w.start()
    acc[...] = jnp.zeros_like(acc)
    ssq[...] = jnp.zeros_like(ssq)
    for i, outer in enumerate(split_taps(lfilt[...].reshape(16, 8, CHAN))):
        for j, inner in enumerate(split_taps(outer)):
            taps[i * 3 + j] = inner

    w_step(0, 1, 0)
    x_step(0, 0)
    y_step(1, 0)
    w_step(0, 1, 1)
    x_step(0, 1)
    y_step(1, 1)
    w_step(0, 2, 0)
    y_step(2, 0)
    w_step(0, 2, 1)
    w_step(0, 3, 0)
    x_step(1, 0)
    y_step(2, 1)
    w_step(0, 3, 1)
    x_step(1, 1)
    to_partner(1, True)
    p_step(0)
    w_step(0, 4, 0)
    w_step(0, 4, 1)
    y_step(3, 0)
    p_step(1)
    w_step(1, 1, 0)
    y_step(3, 1)
    x_step(2, 0)
    local_t.wait()
    local_w.wait()
    column_done(0)
    scale_column(0)
    siblings_done(0)
    products(0, 0)
    w_step(1, 1, 1)
    w_step(1, 2, 0)
    column_done(1)
    scale_column(1)
    x_step(2, 1)
    products(1, 0)
    w_step(1, 2, 1)
    w_step(1, 3, 0)
    column_done(2)
    scale_column(2)
    w_step(1, 3, 1)
    x_step(3, 0)
    x_step(3, 1)
    products(2, 0)
    w_step(1, 4, 0)
    w_step(1, 4, 1)
    siblings_done(1)
    products(0, 1)
    products(1, 1)
    products(2, 1)
    column_done(3)
    scale_column(3)
    products(3, 0)
    products(3, 1)

    scale = lax.rsqrt(jnp.sum(ssq[...], axis=1, keepdims=True) * (1.0 / 8192) + 1e-6)
    projected = (acc[...] * scale).astype(BF16)
    psend[...] = projected[496:512]
    pf[8:520, :] = projected.astype(F32)

    def mixed(start, count, b):
        total = None
        for s in range(SHORT):
            term = sfilt[s, b:b + 1, :] * pf[8 + start - s:8 + start - s + count, b * 256:(b + 1) * 256]
            total = term if total is None else total + term
        return total

    tail = (mixed(384, 128, 1) * mixed(384, 128, 2)).astype(BF16)
    gsend[...] = tail

    def halo(k):
        src, dst = ((gsend, grecv), (psend, precv))[k]
        return pltpu.make_async_remote_copy(
            src_ref=src, dst_ref=dst, send_sem=hss.at[k], recv_sem=hrs.at[k],
            device_id=following, device_id_type=MESH)

    @pl.when(ctx < 31)
    def _():
        halo(0).start()
        halo(1).start()

    def gate(start, count):
        return (mixed(start, count, 1) * mixed(start, count, 2)).astype(BF16).astype(F32)

    gext[144:648, :] = gate(8, 504)
    acc[8:512, 0:256] = mixed(8, 504, 0)
    for b in range(8):
        gsh[b, 144:640] = gext[152 - b:648 - b, :]

    def conv(step, carry):
        row = pl.multiple_of((step // 2) * 128, 128)
        lanes = pl.ds(pl.multiple_of((step % 2) * 128, 128), 128)
        merged = []
        for i in range(3):
            sums = [[None] * 4 for _ in range(3)]
            for b in range(8):
                window = gsh[b, pl.ds(row + 8, 248), lanes]
                tiles = [window[8 * t:8 * t + 8] for t in range(31)]
                for j, part in enumerate(split_tiles(split_tiles(tiles, 16)[i], 8)):
                    for c in range(4):
                        weight = taps[i * 3 + j, c, b:b + 1, lanes]
                        for m in range(4):
                            term = weight * part[m + 3 - c]
                            sums[j][m] = term if sums[j][m] is None else sums[j][m] + term
            merged.append(joined(sums))
        response = jnp.concatenate(joined(merged), axis=0)
        out[pl.ds(row, 128), lanes] = (acc[pl.ds(row, 128), lanes] * response).astype(BF16)
        return carry

    lax.fori_loop(4, 8, conv, 0)

    @pl.when(ctx > 0)
    def _():
        halo(0).wait_recv()
        halo(1).wait_recv()

    @pl.when(ctx == 0)
    def _():
        grecv[...] = jnp.zeros_like(grecv)
        precv[...] = jnp.zeros_like(precv)

    pf[0:8, :] = precv[8:16, :].astype(F32)
    gext[8:136, :] = grecv[...].astype(F32)
    gext[136:144, :] = gate(0, 8)
    acc[0:8, 0:256] = mixed(0, 8, 0)
    for b in range(8):
        gsh[b, 0:144] = gext[8 - b:152 - b, :]

    lax.fori_loop(0, 4, conv, 0)

    for half in range(2):
        if half == 1:
            own_y(half, False)
        to_partner(half, False)
        for n in range(4):
            if n > 0 or half == 1:
                along_x(n, half, False)
            forward_x(n, half, False)
            if n > 0:
                forward_y(n, half, False)
        for stream in range(2):
            for k in range(4):
                if stream + k + half > 0:
                    along_z(stream, k, half, False)
    for stream in range(2):
        for k in range(5):
            to_sibling(stream, k, False)

    @pl.when(ctx < 31)
    def _():
        halo(0).wait_send()
        halo(1).wait_send()


def on_device(tokens, gain, in_weight, short_filter, long_filter):
    vmem = pl.BlockSpec(memory_space=pltpu.VMEM)
    anywhere = pl.BlockSpec(memory_space=pl.ANY)
    dma = pltpu.SemaphoreType.DMA
    return pl.pallas_call(
        kernel,
        out_shape=jax.ShapeDtypeStruct((ROWS, CHAN), BF16),
        in_specs=[anywhere, vmem, anywhere, vmem, vmem],
        out_specs=vmem,
        scratch_shapes=[
            pltpu.VMEM((16, ROWS, FEATS), BF16),
            pltpu.VMEM((16, ROWS, FEATS), BF16),
            pltpu.VMEM((16, 3, 512, CHAN), BF16),
            pltpu.VMEM((ROWS, 3 * CHAN), F32),
            pltpu.VMEM((ROWS, 128), F32),
            pltpu.VMEM((ROWS + 8, 3 * CHAN), F32),
            pltpu.VMEM((ROWS + 136, CHAN), F32),
            pltpu.VMEM((8, ROWS + 128, CHAN), F32),
            pltpu.VMEM((9, 4, 8, CHAN), F32),
            pltpu.VMEM((128, CHAN), BF16),
            pltpu.VMEM((16, 3 * CHAN), BF16),
            pltpu.VMEM((128, CHAN), BF16),
            pltpu.VMEM((16, 3 * CHAN), BF16),
            dma((2,)),
            dma((16, 2, 4)),
            dma((16, 2)),
            dma((32, 2, 4)),
            dma((32, 2)),
            dma((2,)),
            dma((2,)),
        ],
        name="hyena",
        compiler_params=pltpu.CompilerParams(
            collective_id=0, has_side_effects=True, vmem_limit_bytes=56 << 20),
    )(tokens, gain.reshape(1, 8192), in_weight.transpose(1, 0, 2), short_filter, long_filter)


def solution(mesh):
    return jax.shard_map(
        on_device,
        mesh=mesh,
        in_specs=(
            P("ctx", "fsdp"),
            P(),
            P("ctx", None, "fsdp"),
            P(None, None, "fsdp"),
            P(None, "fsdp"),
        ),
        out_specs=P("ctx", "fsdp"),
        check_vma=False,
    )
```

```python
import jax
import jax.numpy as jnp
from jax import lax
from jax.experimental import pallas as pl
from jax.experimental.pallas import tpu as pltpu
from jax.sharding import PartitionSpec as P

MESH = pl.DeviceIdType.MESH
F32 = jnp.float32
BF16 = jnp.bfloat16

ROWS, FEATS, KROWS, CHAN = 512, 512, 256, 256
TAPS, SHORT = 128, 3


def split_taps(values):
    pairs = values.reshape(values.shape[0] // 2, 2, 8, CHAN)
    even, odd = pairs[:, 0], pairs[:, 1]
    return [odd, even + odd, even]


def split_tiles(tiles, count):
    def tile(s):
        return tiles[s + count - 1]

    at = range(1 - count // 2, (len(tiles) - count + 1) // 2)
    return [[tile(2 * m - 1) - tile(2 * m) for m in at], [tile(2 * m) for m in at],
            [tile(2 * m + 1) - tile(2 * m) for m in at]]


def joined(parts):
    result = []
    for before, both, after in zip(*parts):
        result += [both + before, both + after]
    return result


def kernel(tok, gain, w, sfilt, lfilt, out, tall, scaled, wall, acc, ssq, pf, gext, gsh, taps, gsend, psend, grecv, precv,
           lsem, tss, trs, wss, wrs, hss, hrs):
    ctx = lax.axis_index("ctx")
    fsdp = lax.axis_index("fsdp")
    core = ctx % 2
    hi = (ctx // 2) % 2
    z = ctx // 4
    x = fsdp % 4
    lo = fsdp // 4

    def at(xx, ll, hh, zz, cc):
        return ((zz * 2 + hh) * 2 + cc, ll * 4 + xx)

    xp, xm = at((x + 1) % 4, lo, hi, z, core), at((x + 3) % 4, lo, hi, z, core)
    zp, zm = at(x, lo, hi, (z + 1) % 8, core), at(x, lo, hi, (z + 7) % 8, core)
    y = hi * 4 + lo
    yp = at(x, (y + 1) % 8 % 4, (y + 1) % 8 // 4, z, core)
    ym = at(x, (y + 7) % 8 % 4, (y + 7) % 8 // 4, z, core)
    partner = at(x, lo, 1 - hi, z, core)
    sibling = at(x, lo, hi, z, 1 - core)
    following = ((ctx + 1) % 32, fsdp)
    previous = ((ctx + 31) % 32, fsdp)

    barrier = pltpu.get_barrier_semaphore()
    for d in (xp, xm, yp, ym, zp, zm, partner, sibling, previous):
        pl.semaphore_signal(barrier, inc=1, device_id=d, device_id_type=MESH)
    pl.semaphore_wait(barrier, 9)

    def tslice(ref, half):
        return ref.at[pl.ds(half * 256, 256)]

    def tcopy(j, half, way, dest, src=None):
        src = tall.at[j] if src is None else src
        return pltpu.make_async_remote_copy(
            src_ref=tslice(src, half), dst_ref=tslice(tall.at[j], half),
            send_sem=tss.at[j, half, way], recv_sem=trs.at[j, half],
            device_id=dest, device_id_type=MESH)

    def twait(j, half):
        tcopy(j, half, 0, xp).wait_recv()

    me_t = lo * 4 + x
    sent_sign = 3 - 2 * lo
    cols = [lo, lo + 1 - 2 * (lo % 2), 2 - lo // 2, 3 - 3 * (lo // 2)]
    middle = (lo == 1) | (lo == 2)

    def own_y(half, start):
        @pl.when(lo < 3)
        def _():
            c = tcopy(me_t, half, 2, yp, tok)
            c.start() if start else c.wait_send()

        @pl.when(lo > 0)
        def _():
            c = tcopy(me_t, half, 3, ym, tok)
            c.start() if start else c.wait_send()

    def along_x(n, half, start):
        j = cols[n] * 4 + x
        src = tok if n == 0 else None
        for way, dest in ((0, xp), (1, xm)):
            c = tcopy(j, half, way, dest, src)
            c.start() if start else c.wait_send()

    def forward_y(n, half, start):
        j = cols[n] * 4 + x
        sign = sent_sign if n == 1 else -sent_sign

        @pl.when(middle)
        def _():
            dest = at(x, lo + sign, hi, z, core)
            c = tcopy(j, half, 2, dest)
            c.start() if start else c.wait_send()

    def forward_x(n, half, start):
        if half == 0:
            c = tcopy(cols[n] * 4 + (x + 3) % 4, 0, 0, xp)
        else:
            c = tcopy(cols[n] * 4 + (x + 1) % 4, 1, 1, xm)
        c.start() if start else c.wait_send()

    def wpart(i, half):
        return wall.at[i // 2, :, pl.ds(pl.multiple_of((i % 2) * 256 + half * 128, 128), 128)]

    def wfull(i):
        return wall.at[i // 2, :, pl.ds(pl.multiple_of((i % 2) * 256, 256), 256)]

    def wcopy(i, half, way, dest, own=False):
        return pltpu.make_async_remote_copy(
            src_ref=w.at[:, pl.ds(half * 128, 128)] if own else wpart(i, half), dst_ref=wpart(i, half),
            send_sem=wss.at[i, half, way], recv_sem=wrs.at[i, half],
            device_id=dest, device_id_type=MESH)

    def wsib(i, own=False):
        return pltpu.make_async_remote_copy(
            src_ref=w if own else wfull(i), dst_ref=wfull(i), send_sem=wss.at[i, 0, 2], recv_sem=wrs.at[i, 0],
            device_id=sibling, device_id_type=MESH)

    def wid(stream, distance):
        hh = hi if stream == 0 else 1 - hi
        return (((z + 8 + distance) % 8) * 2 + hh) * 2 + core

    def along_z(stream, k, half, start):
        own = stream == 0 and k == 0
        if k <= 2 or half == 0:
            c = wcopy(wid(stream, -k), half, 0, zp, own)
            c.start() if start else c.wait_send()
        if k <= 2 or half == 1:
            c = wcopy(wid(stream, k), half, 1, zm, own)
            c.start() if start else c.wait_send()

    def to_sibling(stream, k, start):
        for distance in sorted({-k, k}) if k < 4 else (4,):
            c = wsib(wid(stream, distance), stream == 0 and k == 0)
            c.start() if start else c.wait_send()

    def to_partner(half, start):
        c = wcopy(ctx, half, 3, partner, True)
        c.start() if start else c.wait_send()

    local_t = pltpu.make_async_copy(tok, tall.at[me_t], lsem.at[0])
    local_w = pltpu.make_async_copy(w, wfull(ctx), lsem.at[1])

    def w_step(stream, k, half):
        if k < 4 or half == 0:
            wcopy(wid(stream, -k), half, 0, zp).wait_recv()
            if k <= 2 or (k == 3 and half == 0):
                wcopy(wid(stream, -k), half, 0, zp).start()
        if k < 4 or half == 1:
            wcopy(wid(stream, k), half, 1, zm).wait_recv()
            if k <= 2 or (k == 3 and half == 1):
                wcopy(wid(stream, k), half, 1, zm).start()
        if half == 1:
            to_sibling(stream, k, True)

    def p_step(half):
        wcopy(wid(1, 0), half, 3, partner).wait_recv()
        along_z(1, 0, half, True)
        if half == 1:
            to_sibling(1, 0, True)

    def y_step(n, half):
        twait(cols[n] * 4 + x, half)
        forward_y(n, half, True)
        along_x(n, half, True)

    def x_step(n, half):
        twait(cols[n] * 4 + ((x + 3) % 4 if half == 0 else (x + 1) % 4), half)
        forward_x(n, half, True)

    def column_done(n):
        twait(cols[n] * 4 + (x + 3) % 4, 1)
        twait(cols[n] * 4 + (x + 1) % 4, 0)
        twait(cols[n] * 4 + (x + 2) % 4, 0)
        twait(cols[n] * 4 + (x + 2) % 4, 1)

    def siblings_done(stream):
        hh = hi if stream == 0 else 1 - hi

        def one(m, carry):
            wsib((m * 2 + hh) * 2 + 1 - core).wait_recv()
            return carry

        lax.fori_loop(0, 8, one, 0)

    def scale_column(n):
        def one(m, carry):
            j = cols[n] * 4 + m
            raw = tall[j].astype(F32)
            sq = raw * raw
            ssq[...] += (sq[:, 0:128] + sq[:, 128:256]) + (sq[:, 256:384] + sq[:, 384:512])
            scaled[j] = (raw * gain[:, pl.ds(pl.multiple_of(j * 512, 512), 512)]).astype(BF16)
            return carry

        lax.fori_loop(0, 4, one, 0)

    def products(n, stream):
        hh = hi if stream == 0 else 1 - hi
        first = cols[n] * 4 + hh
        for b in range(3):
            acc[:, b * 256:(b + 1) * 256] += (
                jnp.dot(scaled[first], wall[first, b], preferred_element_type=F32)
                + jnp.dot(scaled[first + 2], wall[first + 2, b], preferred_element_type=F32))

    for half in range(2):
        if half == 1:
            along_z(0, 0, 0, False)
            along_x(0, 0, False)
        along_z(0, 0, half, True)
        along_x(0, half, True)
        if half == 1:
            own_y(0, False)
        own_y(half, True)
    to_partner(0, True)
    local_t.start()
    local_w.start()
    acc[...] = jnp.zeros_like(acc)
    ssq[...] = jnp.zeros_like(ssq)
    for i, outer in enumerate(split_taps(lfilt[...].reshape(16, 8, CHAN))):
        for j, inner in enumerate(split_taps(outer)):
            taps[i * 3 + j] = inner

    w_step(0, 1, 0)
    x_step(0, 0)
    y_step(1, 0)
    w_step(0, 1, 1)
    x_step(0, 1)
    y_step(1, 1)
    w_step(0, 2, 0)
    y_step(2, 0)
    w_step(0, 2, 1)
    w_step(0, 3, 0)
    x_step(1, 0)
    y_step(2, 1)
    w_step(0, 3, 1)
    x_step(1, 1)
    to_partner(1, True)
    p_step(0)
    w_step(0, 4, 0)
    w_step(0, 4, 1)
    to_sibling(0, 0, True)
    y_step(3, 0)
    p_step(1)
    w_step(1, 1, 0)
    y_step(3, 1)
    x_step(2, 0)
    local_t.wait()
    local_w.wait()
    column_done(0)
    scale_column(0)
    siblings_done(0)
    products(0, 0)
    w_step(1, 1, 1)
    w_step(1, 2, 0)
    column_done(1)
    scale_column(1)
    x_step(2, 1)
    products(1, 0)
    w_step(1, 2, 1)
    w_step(1, 3, 0)
    column_done(2)
    scale_column(2)
    w_step(1, 3, 1)
    x_step(3, 0)
    x_step(3, 1)
    products(2, 0)
    w_step(1, 4, 0)
    w_step(1, 4, 1)
    siblings_done(1)
    products(0, 1)
    products(1, 1)
    products(2, 1)
    column_done(3)
    scale_column(3)
    products(3, 0)
    products(3, 1)

    scale = lax.rsqrt(jnp.sum(ssq[...], axis=1, keepdims=True) * (1.0 / 8192) + 1e-6)
    projected = (acc[...] * scale).astype(BF16)
    psend[...] = projected[496:512]
    pf[8:520, :] = projected.astype(F32)

    def mixed(start, count, b):
        total = None
        for s in range(SHORT):
            term = sfilt[s, b:b + 1, :] * pf[8 + start - s:8 + start - s + count, b * 256:(b + 1) * 256]
            total = term if total is None else total + term
        return total

    tail = (mixed(384, 128, 1) * mixed(384, 128, 2)).astype(BF16)
    gsend[...] = tail

    def halo(k):
        src, dst = ((gsend, grecv), (psend, precv))[k]
        return pltpu.make_async_remote_copy(
            src_ref=src, dst_ref=dst, send_sem=hss.at[k], recv_sem=hrs.at[k],
            device_id=following, device_id_type=MESH)

    @pl.when(ctx < 31)
    def _():
        halo(0).start()
        halo(1).start()

    def gate(start, count):
        return (mixed(start, count, 1) * mixed(start, count, 2)).astype(BF16).astype(F32)

    gext[144:648, :] = gate(8, 504)
    acc[8:512, 0:256] = mixed(8, 504, 0)
    for b in range(8):
        gsh[b, 144:640] = gext[152 - b:648 - b, :]

    def conv(step, carry):
        row = pl.multiple_of((step // 2) * 128, 128)
        lanes = pl.ds(pl.multiple_of((step % 2) * 128, 128), 128)
        merged = []
        for i in range(3):
            sums = [[None] * 4 for _ in range(3)]
            for b in range(8):
                window = gsh[b, pl.ds(row + 8, 248), lanes]
                tiles = [window[8 * t:8 * t + 8] for t in range(31)]
                for j, part in enumerate(split_tiles(split_tiles(tiles, 16)[i], 8)):
                    for c in range(4):
                        weight = taps[i * 3 + j, c, b:b + 1, lanes]
                        for m in range(4):
                            term = weight * part[m + 3 - c]
                            sums[j][m] = term if sums[j][m] is None else sums[j][m] + term
            merged.append(joined(sums))
        response = jnp.concatenate(joined(merged), axis=0)
        out[pl.ds(row, 128), lanes] = (acc[pl.ds(row, 128), lanes] * response).astype(BF16)
        return carry

    lax.fori_loop(4, 8, conv, 0)

    @pl.when(ctx > 0)
    def _():
        halo(0).wait_recv()
        halo(1).wait_recv()

    @pl.when(ctx == 0)
    def _():
        grecv[...] = jnp.zeros_like(grecv)
        precv[...] = jnp.zeros_like(precv)

    pf[0:8, :] = precv[8:16, :].astype(F32)
    gext[8:136, :] = grecv[...].astype(F32)
    gext[136:144, :] = gate(0, 8)
    acc[0:8, 0:256] = mixed(0, 8, 0)
    for b in range(8):
        gsh[b, 0:144] = gext[8 - b:152 - b, :]

    lax.fori_loop(0, 4, conv, 0)

    for half in range(2):
        if half == 1:
            own_y(half, False)
        to_partner(half, False)
        for n in range(4):
            if n > 0 or half == 1:
                along_x(n, half, False)
            forward_x(n, half, False)
            if n > 0:
                forward_y(n, half, False)
        for stream in range(2):
            for k in range(4):
                if stream + k + half > 0:
                    along_z(stream, k, half, False)
    for stream in range(2):
        for k in range(5):
            to_sibling(stream, k, False)

    @pl.when(ctx < 31)
    def _():
        halo(0).wait_send()
        halo(1).wait_send()


def on_device(tokens, gain, in_weight, short_filter, long_filter):
    vmem = pl.BlockSpec(memory_space=pltpu.VMEM)
    anywhere = pl.BlockSpec(memory_space=pl.ANY)
    dma = pltpu.SemaphoreType.DMA
    return pl.pallas_call(
        kernel,
        out_shape=jax.ShapeDtypeStruct((ROWS, CHAN), BF16),
        in_specs=[anywhere, vmem, anywhere, vmem, vmem],
        out_specs=vmem,
        scratch_shapes=[
            pltpu.VMEM((16, ROWS, FEATS), BF16),
            pltpu.VMEM((16, ROWS, FEATS), BF16),
            pltpu.VMEM((16, 3, 512, CHAN), BF16),
            pltpu.VMEM((ROWS, 3 * CHAN), F32),
            pltpu.VMEM((ROWS, 128), F32),
            pltpu.VMEM((ROWS + 8, 3 * CHAN), F32),
            pltpu.VMEM((ROWS + 136, CHAN), F32),
            pltpu.VMEM((8, ROWS + 128, CHAN), F32),
            pltpu.VMEM((9, 4, 8, CHAN), F32),
            pltpu.VMEM((128, CHAN), BF16),
            pltpu.VMEM((16, 3 * CHAN), BF16),
            pltpu.VMEM((128, CHAN), BF16),
            pltpu.VMEM((16, 3 * CHAN), BF16),
            dma((2,)),
            dma((16, 2, 4)),
            dma((16, 2)),
            dma((32, 2, 4)),
            dma((32, 2)),
            dma((2,)),
            dma((2,)),
        ],
        name="hyena",
        compiler_params=pltpu.CompilerParams(
            collective_id=0, has_side_effects=True, vmem_limit_bytes=56 << 20),
    )(tokens, gain.reshape(1, 8192), in_weight.transpose(1, 0, 2), short_filter, long_filter)


def solution(mesh):
    return jax.shard_map(
        on_device,
        mesh=mesh,
        in_specs=(
            P("ctx", "fsdp"),
            P(),
            P("ctx", None, "fsdp"),
            P(None, None, "fsdp"),
            P(None, "fsdp"),
        ),
        out_specs=P("ctx", "fsdp"),
        check_vma=False,
    )
```
